32 devices in a mesh: row: 8 (over z, core), col: 4 (over y, x).
Axes of the slice: x: 2, y: 2, z: 4, core: 2. Of those that a mesh axis runs over, the one named last changes fastest.
Arguments:
- roll_hidden: bfloat16 [1344, 4096], P(('row', 'col')), may hold values from -6 to 6
- roll_cotangent: bfloat16 [1344, 4096], P(('row', 'col')), may hold values from -6 to 6
- lengths: int32 [32], P(('row', 'col')), may hold values from 1 to 42, as said below
- owners: int32 [32], P(('row', 'col')), may hold values from 0 to 7, as said below
- prompts: int32 [32], P(('row', 'col')), may hold values from 0 to 3
- rewards: float32 [32], P(('row', 'col')), may hold values from -5 to 5
- gate_weight: bfloat16 [4096, 14784], P('col', 'row'), may hold values from -0.09375 to 0.09375
- up_weight: bfloat16 [4096, 14784], P('col', 'row'), may hold values from -0.09375 to 0.09375
- down_weight: bfloat16 [14784, 4096], P('row', 'col'), may hold values from -0.046875 to 0.046875
Outputs:
- grad_input: bfloat16 [1024, 4096], P('row', 'col')
- grad_gate: bfloat16 [4096, 14784], P('col', 'row')
- grad_up: bfloat16 [4096, 14784], P('col', 'row')
- grad_down: bfloat16 [14784, 4096], P('row', 'col')
The draws below stay inside these ranges and needn't reach their ends.
Inputs may be any that keep to these rules, and one draw needn't show every extreme that they name: `owners`: each owner value names exactly 4 rows; the lengths of one owner's rows sum to at most 128, and to exactly 128 for some owner in every draw. `lengths`: some row has length 42 in every draw.
All inputs are finite; a program needn't handle non-finite values.
Results may differ from the reference program's by a relative error of at most 0.025.
Values may be sent and summed in bfloat16 or wider, within the bound.
A program may use at most 128 MiB of HBM per device.

```python
import jax
import jax.numpy as jnp
from jax import lax

D = 4096
FF = 14784
CAPR = 128
MAXLEN = 42
OWNERS = 8
PER_OWNER = 4
ROWS = 32
PROMPTS = 4
TOKENS = 1024
N_COL = 4


def owner_table(key):
    key_perm = jax.random.fold_in(key, 101)
    key_special = jax.random.fold_in(key, 202)
    key_total = jax.random.fold_in(key, 303)
    key_share = jax.random.fold_in(key, 404)
    order = jax.random.permutation(key_perm, ROWS).astype(jnp.int32)
    owner = (order // PER_OWNER).astype(jnp.int32)
    place = (order % PER_OWNER).astype(jnp.int32)
    special = jax.random.randint(key_special, (), 0, OWNERS, dtype=jnp.int32)
    ids = jnp.arange(OWNERS, dtype=jnp.int32)
    total = jax.random.randint(key_total, (OWNERS,), CAPR // 2, CAPR + 1, dtype=jnp.int32)
    total = jnp.where(ids == special, CAPR, total)
    has_big = (ids == special).astype(jnp.int32)
    columns = jnp.arange(PER_OWNER, dtype=jnp.int32)
    is_big = (has_big[:, None] == 1) & (columns[None, :] == 0)
    shares = jax.random.randint(key_share, (OWNERS, PER_OWNER), 1, 4, dtype=jnp.int32)
    shares = jnp.where(has_big[:, None] == 1, 1, shares)
    shares = jnp.where(is_big, 0, shares)
    share_sum = jnp.sum(shares, 1)
    small_count = PER_OWNER - has_big
    extra = total - has_big * MAXLEN - small_count
    portion = extra[:, None] * shares // share_sum[:, None]
    remain = extra - jnp.sum(portion, 1)
    ranks = columns[None, :] - has_big[:, None]
    bump = ((ranks < remain[:, None]) & jnp.logical_not(is_big)).astype(jnp.int32)
    raw = jnp.minimum(1 + portion + bump, MAXLEN)
    parts = jnp.where(is_big, MAXLEN, raw).astype(jnp.int32)
    lengths = parts[owner, place].astype(jnp.int32)
    return (lengths, owner)


def draw_lengths(key, part):
    return owner_table(key)[0]


def draw_owners(key, part):
    return owner_table(key)[1]


def place_ends(entries, key, least, largest):
    longest = entries.shape.index(max(entries.shape))
    spots = []
    for shift in (0, 1):
        where = [jax.random.randint(jax.random.fold_in(key, axis), (), 0, length) for axis, length in enumerate(entries.shape)]
        where[longest] = (where[longest] + shift) % entries.shape[longest]
        spots.append(tuple(where))
    return entries.at[spots[0]].set(least).at[spots[1]].set(largest)


def block_scale(stream_key, dims, split, smallest, top_value):
    gain, own = 1.0, jax.random.fold_in(stream_key, 6)
    for axis_at, blocks in split:
        draws = jnp.exp(jax.random.uniform(jax.random.fold_in(own, axis_at), (blocks,), jnp.float32, smallest / len(split), top_value / len(split)))
        gain = gain * jnp.repeat(draws, dims[axis_at] // blocks).reshape([-1 if axis == axis_at else 1 for axis in range(len(dims))])
    return gain


def normal_values(key, shape, deviation, most, pieces=(), kind=jnp.bfloat16):
    values = deviation * jax.random.normal(key, shape, jnp.float32)
    if pieces:
        values = values * block_scale(key, shape, pieces, -0.22, 0.18)
    return jnp.clip(values, -most, most).astype(kind)


def setup_inputs(seed: int = 0) -> dict:
    streams_of = jax.random.split(jax.random.key(seed), 10)
    roll_hidden = normal_values(streams_of[0], (ROWS * MAXLEN, D), 1.0, 6.0, ((0, 32),))
    roll_cotangent = normal_values(streams_of[1], (ROWS * MAXLEN, D), 1.0, 6.0, ((0, 32),))
    lengths = draw_lengths(jax.random.fold_in(streams_of[9], 71), 0)
    owners = draw_owners(jax.random.fold_in(streams_of[9], 71), 0)
    prompts = place_ends(jax.random.randint(streams_of[4], (ROWS,), 0, PROMPTS), jax.random.fold_in(streams_of[4], 1), 0, PROMPTS - 1).astype(jnp.int32)
    rewards = normal_values(streams_of[5], (ROWS,), 1.0, 5.0, ((0, 32),), jnp.float32)
    gate_weight = normal_values(streams_of[6], (D, FF), D ** -0.5, 0.09375, ((0, 4), (1, 8)))
    up_weight = normal_values(streams_of[7], (D, FF), D ** -0.5, 0.09375, ((0, 4), (1, 8)))
    down_weight = normal_values(streams_of[8], (FF, D), FF ** -0.5, 0.046875, ((0, 8), (1, 4)))
    return {"roll_hidden": roll_hidden, "roll_cotangent": roll_cotangent, "lengths": lengths, "owners": owners, "prompts": prompts, "rewards": rewards, "gate_weight": gate_weight, "up_weight": up_weight, "down_weight": down_weight}


spread_floor = 0.7

def row_weights(lengths, prompts, rewards, count_prompts):
    onehot = (prompts[:, None] == jnp.arange(count_prompts, dtype=jnp.int32)[None, :]).astype(jnp.float32)
    counts = jnp.maximum(lax.optimization_barrier(jnp.sum(onehot, 0)), 1.0)
    means = lax.optimization_barrier(jnp.sum(onehot * rewards[:, None], 0)) / counts
    centred = rewards - lax.optimization_barrier(jnp.sum(onehot * means[None, :], 1))
    spreads = jnp.sqrt(lax.optimization_barrier(jnp.sum(onehot * (centred * centred)[:, None], 0)) / counts)
    divisor = jnp.maximum(lax.optimization_barrier(jnp.sum(onehot * spreads[None, :], 1)), spread_floor)
    return centred / divisor / lengths.astype(jnp.float32)

def row_offsets(lengths, owners):
    count = lengths.shape[0]
    places = jnp.arange(count, dtype=jnp.int32)
    earlier = (owners[None, :] == owners[:, None]) & (places[None, :] < places[:, None])
    return lax.optimization_barrier(jnp.sum(jnp.where(earlier, lengths[None, :], 0), 1)).astype(jnp.int32)

def block_sum(left, right, blocks, transpose_right):
    width = left.shape[1] // blocks
    total = None
    for index in range(blocks):
        piece = left[:, index * width:(index + 1) * width]
        if transpose_right:
            other = right[:, index * width:(index + 1) * width]
            term = lax.dot_general(piece, other, (((1,), (1,)), ((), ())), preferred_element_type=jnp.float32)
        else:
            other = right[index * width:(index + 1) * width, :]
            term = jnp.dot(piece, other, preferred_element_type=jnp.float32)
        term = lax.optimization_barrier(term.astype(jnp.bfloat16)).astype(jnp.float32)
        total = term if total is None else total + term
    return total

def reference(roll_hidden, roll_cotangent, lengths, owners, prompts, rewards, gate_weight, up_weight, down_weight):
    weight = row_weights(lengths, prompts, rewards, PROMPTS)
    offsets = row_offsets(lengths, owners)
    slots = jnp.arange(MAXLEN, dtype=jnp.int32)
    live = slots[None, :] < lengths[:, None]
    target = jnp.where(live, owners[:, None] * CAPR + offsets[:, None] + slots[None, :], TOKENS).astype(jnp.int32)
    hidden_rows = roll_hidden.reshape(ROWS, MAXLEN, D)
    cot_rows = roll_cotangent.reshape(ROWS, MAXLEN, D).astype(jnp.float32)
    upstream = jnp.where(live[:, :, None], cot_rows * weight[:, None, None], 0.0).astype(jnp.bfloat16)
    flat_target = target.reshape(-1)
    packed = jnp.zeros((TOKENS, D), jnp.bfloat16).at[flat_target].set(hidden_rows.reshape(-1, D), mode='drop')
    packed_grad = jnp.zeros((TOKENS, D), jnp.bfloat16).at[flat_target].set(upstream.reshape(-1, D), mode='drop')
    gate = block_sum(packed, gate_weight, N_COL, False)
    upval = block_sum(packed, up_weight, N_COL, False)
    sig = jax.nn.sigmoid(gate)
    silu = gate * sig
    hidden = (silu * upval).astype(jnp.bfloat16)
    grad_hidden = block_sum(packed_grad, down_weight, N_COL, True)
    grad_gate_act = (grad_hidden * upval * sig * (1.0 + gate * (1.0 - sig))).astype(jnp.bfloat16)
    grad_up_act = (grad_hidden * silu).astype(jnp.bfloat16)
    contract_rows = (((0,), (0,)), ((), ()))
    grad_down = lax.dot_general(hidden, packed_grad, contract_rows, preferred_element_type=jnp.float32).astype(jnp.bfloat16)
    grad_gate = lax.dot_general(packed, grad_gate_act, contract_rows, preferred_element_type=jnp.float32).astype(jnp.bfloat16)
    grad_up = lax.dot_general(packed, grad_up_act, contract_rows, preferred_element_type=jnp.float32).astype(jnp.bfloat16)
    contract_cols = (((1,), (1,)), ((), ()))
    grad_input = lax.dot_general(grad_gate_act, gate_weight, contract_cols, preferred_element_type=jnp.float32)
    grad_input = grad_input + lax.dot_general(grad_up_act, up_weight, contract_cols, preferred_element_type=jnp.float32)
    return (grad_input.astype(jnp.bfloat16), grad_gate, grad_up, grad_down)
```

```python
import functools

import jax
import jax.numpy as jnp
from jax import lax
from jax.experimental import pallas as pl
from jax.experimental.pallas import tpu as pltpu
from jax.sharding import PartitionSpec as P

CAPR = 128
MESH = pl.DeviceIdType.MESH
CHUNK = 256


spread_floor = 0.7


def row_weights(lengths, prompts, rewards, count_prompts):
    onehot = (prompts[:, None] == jnp.arange(count_prompts, dtype=jnp.int32)[None, :]).astype(
        jnp.float32
    )
    counts = jnp.maximum(jnp.sum(onehot, 0), 1.0)
    means = jnp.sum(onehot * rewards[:, None], 0) / counts
    centred = rewards - jnp.sum(onehot * means[None, :], 1)
    spreads = jnp.sqrt(jnp.sum(onehot * (centred * centred)[:, None], 0) / counts)
    divisor = jnp.maximum(jnp.sum(onehot * spreads[None, :], 1), spread_floor)
    return centred / divisor / lengths.astype(jnp.float32)


def row_offsets(lengths, owners):
    count = lengths.shape[0]
    places = jnp.arange(count, dtype=jnp.int32)
    earlier = (owners[None, :] == owners[:, None]) & (places[None, :] < places[:, None])
    return jnp.sum(jnp.where(earlier, lengths[None, :], 0), 1)


def square_kernel(count, transposed, a_ref, *refs):
    b_refs, o_refs = refs[:count], refs[count : 2 * count]
    parts, first_in, second_out, second_in = (
        refs[2 * count + i * count : 3 * count + i * count] for i in range(4)
    )
    send_sem, recv_sem = refs[6 * count :]
    col = lax.axis_index("col")
    row = lax.axis_index("row")
    x, y = lax.rem(col, 2), lax.div(col, 2)
    x_peer, y_peer = y * 2 + (1 - x), (1 - y) * 2 + x
    half, quarter, eighth = CHUNK // 2, CHUNK // 4, CHUNK // 8
    ways = ((x, y, x_peer, y_peer), (y, x, y_peer, x_peer))
    chunks = a_ref.shape[0] // CHUNK

    barrier = pltpu.get_barrier_semaphore()
    for peer in (x_peer, y_peer):
        pl.semaphore_signal(barrier, inc=1, device_id=(row, peer), device_id_type=MESH)
    pl.semaphore_wait(barrier, 2)

    def rows(start, size):
        return pl.ds(pl.multiple_of(start, eighth), size)

    def copy(stage, chunk, way, i):
        f, s, f_peer, s_peer = ways[way]
        base = chunk * CHUNK + way * half
        if stage == 0:
            src = parts[i].at[rows(base + (1 - f) * quarter, quarter)]
            dst = first_in[i].at[rows(chunk * half + way * quarter, quarter)]
        elif stage == 1:
            place = rows(chunk * quarter + way * eighth, eighth)
            src, dst = second_out[i].at[place], second_in[i].at[place]
        elif stage == 2:
            place = rows(base + f * quarter + s * eighth, eighth)
            src = dst = o_refs[i].at[place]
        else:
            place = rows(base + f * quarter, quarter)
            src = dst = o_refs[i].at[place]
        return pltpu.make_async_remote_copy(
            src_ref=src,
            dst_ref=dst,
            send_sem=send_sem.at[stage, way, i, chunk],
            recv_sem=recv_sem.at[stage, way, i, chunk],
            device_id=(row, f_peer if stage in (0, 3) else s_peer),
            device_id_type=MESH,
        )

    def phase_first(chunk, carry):
        block = a_ref[rows(chunk * CHUNK, CHUNK), :]
        dims = (((1,), (1 if transposed else 0,)), ((), ()))
        for i in range(count):
            parts[i][rows(chunk * CHUNK, CHUNK), :] = lax.dot_general(
                block, b_refs[i][...], dims, preferred_element_type=jnp.float32
            ).astype(jnp.bfloat16)
            for way in range(2):
                copy(0, chunk, way, i).start()
        return carry

    def phase_second(chunk, carry):
        for i in range(count):
            for way in range(2):
                f, s = ways[way][:2]
                copy(0, chunk, way, i).wait_recv()
                mine = parts[i][
                    rows(chunk * CHUNK + way * half + f * quarter + (1 - s) * eighth, eighth), :
                ]
                other = first_in[i][
                    rows(chunk * half + way * quarter + (1 - s) * eighth, eighth), :
                ]
                second_out[i][rows(chunk * quarter + way * eighth, eighth), :] = (
                    mine.astype(jnp.float32) + other.astype(jnp.float32)
                ).astype(jnp.bfloat16)
                copy(1, chunk, way, i).start()
        return carry

    def phase_third(chunk, carry):
        for i in range(count):
            for way in range(2):
                f, s = ways[way][:2]
                copy(1, chunk, way, i).wait_recv()
                place = rows(chunk * CHUNK + way * half + f * quarter + s * eighth, eighth)
                mine = parts[i][place, :].astype(jnp.float32)
                other = first_in[i][
                    rows(chunk * half + way * quarter + s * eighth, eighth), :
                ].astype(jnp.float32)
                pair = second_in[i][rows(chunk * quarter + way * eighth, eighth), :].astype(
                    jnp.float32
                )
                o_refs[i][place, :] = (mine + other + pair).astype(jnp.bfloat16)
                copy(2, chunk, way, i).start()
        return carry

    def phase_fourth(chunk, carry):
        for i in range(count):
            for way in range(2):
                copy(2, chunk, way, i).wait_recv()
                copy(3, chunk, way, i).start()
        return carry

    def phase_last(chunk, carry):
        for i in range(count):
            for way in range(2):
                copy(3, chunk, way, i).wait_recv()
                for stage in range(4):
                    copy(stage, chunk, way, i).wait_send()
        return carry

    for phase in (phase_first, phase_second, phase_third, phase_fourth, phase_last):
        lax.fori_loop(0, chunks, phase, 0)


def square_sum(a, bs, transposed, collective_id):
    tokens, depth = a.shape
    units = bs[0].shape[0 if transposed else 1]
    count = len(bs)
    shapes = (tokens, tokens // 2, tokens // 4, tokens // 4)
    return pl.pallas_call(
        functools.partial(square_kernel, count, transposed),
        out_shape=[jax.ShapeDtypeStruct((tokens, units), jnp.bfloat16)] * count,
        in_specs=[pl.BlockSpec(memory_space=pltpu.VMEM)] * (1 + count),
        out_specs=[pl.BlockSpec(memory_space=pltpu.VMEM)] * count,
        scratch_shapes=[
            pltpu.VMEM((size, units), jnp.bfloat16) for size in shapes for _ in range(count)
        ]
        + [pltpu.SemaphoreType.DMA((4, 2, count, tokens // CHUNK))] * 2,
        compiler_params=pltpu.CompilerParams(
            collective_id=collective_id, has_side_effects=True, vmem_limit_bytes=56 * 1024 * 1024
        ),
        cost_estimate=pl.CostEstimate(
            flops=2 * count * tokens * depth * units * 6,
            bytes_accessed=60 * count * tokens * units,
            transcendentals=0,
        ),
    )(a, *bs)


def column_sum(a, bs, transposed, collective_id):
    if lax.axis_size("col") == 4 and a.shape[0] % CHUNK == 0:
        return square_sum(a, bs, transposed, collective_id)
    dims = (((1,), (1 if transposed else 0,)), ((), ()))
    return [
        lax.psum(
            lax.dot_general(a, b, dims, preferred_element_type=jnp.float32).astype(jnp.bfloat16),
            "col",
        )
        for b in bs
    ]


def per_device(
    roll_hidden,
    roll_cotangent,
    lengths,
    owners,
    prompts,
    rewards,
    gate_weight,
    up_weight,
    down_weight,
):
    row_count = lax.axis_size("row")
    col_count = lax.axis_size("col")
    total_tokens = row_count * CAPR
    count_prompts = row_count * col_count // 8
    slot_count = roll_hidden.shape[0]
    width = roll_hidden.shape[1] // col_count
    local = jnp.stack(
        [
            lengths.astype(jnp.float32),
            owners.astype(jnp.float32),
            prompts.astype(jnp.float32),
            rewards,
        ],
        axis=1,
    )
    table = lax.all_gather(local, ("row", "col"), axis=0, tiled=True)
    all_lengths = table[:, 0].astype(jnp.int32)
    all_owners = table[:, 1].astype(jnp.int32)
    all_prompts = table[:, 2].astype(jnp.int32)
    weights = row_weights(all_lengths, all_prompts, table[:, 3], count_prompts)
    offsets = row_offsets(all_lengths, all_owners)
    slots = jnp.arange(slot_count, dtype=jnp.int32)
    target = jnp.where(
        slots[None, :] < all_lengths[:, None],
        all_owners[:, None] * CAPR + offsets[:, None] + slots[None, :],
        total_tokens,
    ).reshape(-1)
    slot_weights = jnp.repeat(weights, slot_count)
    pick = (jnp.arange(total_tokens, dtype=jnp.int32)[:, None] == target[None, :]).astype(
        jnp.bfloat16
    )

    def to_cols(rolled):
        blocks = rolled.reshape(slot_count, col_count, width)
        return lax.all_to_all(blocks, "col", split_axis=1, concat_axis=0, tiled=True).reshape(
            col_count * slot_count, width
        )

    def repack(every):
        return jnp.dot(pick, every, preferred_element_type=jnp.float32).astype(jnp.bfloat16)

    hidden_cols, table = lax.optimization_barrier((to_cols(roll_hidden), table))
    hidden_all = lax.all_gather(hidden_cols, "row", axis=0, tiled=True)
    cotangent_all = lax.all_gather(to_cols(roll_cotangent), "row", axis=0, tiled=True)
    packed = repack(hidden_all)
    gate, upval = column_sum(packed, (gate_weight, up_weight), False, 0)
    packed_grad = repack(
        (cotangent_all.astype(jnp.float32) * slot_weights[:, None]).astype(jnp.bfloat16)
    )
    (grad_hidden,) = column_sum(packed_grad, (down_weight,), True, 1)
    gate, upval, grad_hidden = (v.astype(jnp.float32) for v in (gate, upval, grad_hidden))
    sig = jax.nn.sigmoid(gate)
    silu = gate * sig
    hidden = (silu * upval).astype(jnp.bfloat16)
    contract_cols = (((1,), (1,)), ((), ()))
    grad_gate_act = (grad_hidden * upval * sig * (1.0 + gate * (1.0 - sig))).astype(jnp.bfloat16)
    grad_up_act = (grad_hidden * silu).astype(jnp.bfloat16)
    contract_rows = (((0,), (0,)), ((), ()))
    grad_down = lax.dot_general(
        hidden, packed_grad, contract_rows, preferred_element_type=jnp.float32
    ).astype(jnp.bfloat16)
    grad_gate = lax.dot_general(
        packed, grad_gate_act, contract_rows, preferred_element_type=jnp.float32
    ).astype(jnp.bfloat16)
    grad_up = lax.dot_general(
        packed, grad_up_act, contract_rows, preferred_element_type=jnp.float32
    ).astype(jnp.bfloat16)
    term = lax.dot_general(
        grad_gate_act, gate_weight, contract_cols, preferred_element_type=jnp.float32
    )
    grad_input = lax.psum_scatter(
        (
            term
            + lax.dot_general(
                grad_up_act, up_weight, contract_cols, preferred_element_type=jnp.float32
            )
        ).astype(jnp.bfloat16),
        "row",
        scatter_dimension=0,
        tiled=True,
    )
    return (grad_input, grad_gate, grad_up, grad_down)


def solution(mesh):
    return jax.shard_map(
        per_device,
        mesh=mesh,
        in_specs=(
            P(("row", "col"), None),
            P(("row", "col"), None),
            P(("row", "col")),
            P(("row", "col")),
            P(("row", "col")),
            P(("row", "col")),
            P("col", "row"),
            P("col", "row"),
            P("row", "col"),
        ),
        out_specs=(P("row", "col"), P("col", "row"), P("col", "row"), P("row", "col")),
        check_vma=False,
    )
```

```python
import functools

import jax
import jax.numpy as jnp
from jax import lax
from jax.experimental import pallas as pl
from jax.experimental.pallas import tpu as pltpu
from jax.sharding import PartitionSpec as P

CAPR = 128
MESH = pl.DeviceIdType.MESH
CHUNK = 256


spread_floor = 0.7


def row_weights(lengths, prompts, rewards, count_prompts):
    onehot = (prompts[:, None] == jnp.arange(count_prompts, dtype=jnp.int32)[None, :]).astype(
        jnp.float32
    )
    counts = jnp.maximum(jnp.sum(onehot, 0), 1.0)
    means = jnp.sum(onehot * rewards[:, None], 0) / counts
    centred = rewards - jnp.sum(onehot * means[None, :], 1)
    spreads = jnp.sqrt(jnp.sum(onehot * (centred * centred)[:, None], 0) / counts)
    divisor = jnp.maximum(jnp.sum(onehot * spreads[None, :], 1), spread_floor)
    return centred / divisor / lengths.astype(jnp.float32)


def row_offsets(lengths, owners):
    count = lengths.shape[0]
    places = jnp.arange(count, dtype=jnp.int32)
    earlier = (owners[None, :] == owners[:, None]) & (places[None, :] < places[:, None])
    return jnp.sum(jnp.where(earlier, lengths[None, :], 0), 1)


def square_kernel(count, a_ref, *refs):
    b_refs, o_refs = refs[:count], refs[count : 2 * count]
    parts, first_in, second_out, second_in = (
        refs[2 * count + i * count : 3 * count + i * count] for i in range(4)
    )
    send_sem, recv_sem = refs[6 * count :]
    col = lax.axis_index("col")
    row = lax.axis_index("row")
    x, y = lax.rem(col, 2), lax.div(col, 2)
    x_peer, y_peer = y * 2 + (1 - x), (1 - y) * 2 + x
    half, quarter, eighth = CHUNK // 2, CHUNK // 4, CHUNK // 8
    ways = ((x, y, x_peer, y_peer), (y, x, y_peer, x_peer))
    chunks = a_ref.shape[0] // CHUNK

    barrier = pltpu.get_barrier_semaphore()
    for peer in (x_peer, y_peer):
        pl.semaphore_signal(barrier, inc=1, device_id=(row, peer), device_id_type=MESH)
    pl.semaphore_wait(barrier, 2)

    def rows(start, size):
        return pl.ds(pl.multiple_of(start, eighth), size)

    def copy(stage, chunk, way, i):
        f, s, f_peer, s_peer = ways[way]
        base = chunk * CHUNK + way * half
        if stage == 0:
            src = parts[i].at[rows(base + (1 - f) * quarter, quarter)]
            dst = first_in[i].at[rows(chunk * half + way * quarter, quarter)]
        elif stage == 1:
            place = rows(chunk * quarter + way * eighth, eighth)
            src, dst = second_out[i].at[place], second_in[i].at[place]
        elif stage == 2:
            place = rows(base + f * quarter + s * eighth, eighth)
            src = dst = o_refs[i].at[place]
        else:
            place = rows(base + f * quarter, quarter)
            src = dst = o_refs[i].at[place]
        return pltpu.make_async_remote_copy(
            src_ref=src,
            dst_ref=dst,
            send_sem=send_sem.at[stage, way, i, chunk],
            recv_sem=recv_sem.at[stage, way, i, chunk],
            device_id=(row, f_peer if stage in (0, 3) else s_peer),
            device_id_type=MESH,
        )

    def phase_first(chunk, carry):
        block = a_ref[rows(chunk * CHUNK, CHUNK), :]
        dims = (((1,), (1,)), ((), ()))
        for i in range(count):
            parts[i][rows(chunk * CHUNK, CHUNK), :] = lax.dot_general(
                block, b_refs[i][...], dims, preferred_element_type=jnp.float32
            ).astype(jnp.bfloat16)
            for way in range(2):
                copy(0, chunk, way, i).start()
        return carry

    def phase_second(chunk, carry):
        for i in range(count):
            for way in range(2):
                f, s = ways[way][:2]
                copy(0, chunk, way, i).wait_recv()
                mine = parts[i][
                    rows(chunk * CHUNK + way * half + f * quarter + (1 - s) * eighth, eighth), :
                ]
                other = first_in[i][
                    rows(chunk * half + way * quarter + (1 - s) * eighth, eighth), :
                ]
                second_out[i][rows(chunk * quarter + way * eighth, eighth), :] = (
                    mine.astype(jnp.float32) + other.astype(jnp.float32)
                ).astype(jnp.bfloat16)
                copy(1, chunk, way, i).start()
        return carry

    def phase_third(chunk, carry):
        for i in range(count):
            for way in range(2):
                f, s = ways[way][:2]
                copy(1, chunk, way, i).wait_recv()
                place = rows(chunk * CHUNK + way * half + f * quarter + s * eighth, eighth)
                mine = parts[i][place, :].astype(jnp.float32)
                other = first_in[i][
                    rows(chunk * half + way * quarter + s * eighth, eighth), :
                ].astype(jnp.float32)
                pair = second_in[i][rows(chunk * quarter + way * eighth, eighth), :].astype(
                    jnp.float32
                )
                o_refs[i][place, :] = (mine + other + pair).astype(jnp.bfloat16)
                copy(2, chunk, way, i).start()
        return carry

    def phase_fourth(chunk, carry):
        for i in range(count):
            for way in range(2):
                copy(2, chunk, way, i).wait_recv()
                copy(3, chunk, way, i).start()
        return carry

    def phase_last(chunk, carry):
        for i in range(count):
            for way in range(2):
                copy(3, chunk, way, i).wait_recv()
                for stage in range(4):
                    copy(stage, chunk, way, i).wait_send()
        return carry

    for phase in (phase_first, phase_second, phase_third, phase_fourth, phase_last):
        lax.fori_loop(0, chunks, phase, 0)


def square_sum(a, bs, collective_id):
    tokens, depth = a.shape
    units = bs[0].shape[0]
    count = len(bs)
    shapes = (tokens, tokens // 2, tokens // 4, tokens // 4)
    return pl.pallas_call(
        functools.partial(square_kernel, count),
        out_shape=[jax.ShapeDtypeStruct((tokens, units), jnp.bfloat16)] * count,
        in_specs=[pl.BlockSpec(memory_space=pltpu.VMEM)] * (1 + count),
        out_specs=[pl.BlockSpec(memory_space=pltpu.VMEM)] * count,
        scratch_shapes=[
            pltpu.VMEM((size, units), jnp.bfloat16) for size in shapes for _ in range(count)
        ]
        + [pltpu.SemaphoreType.DMA((4, 2, count, tokens // CHUNK))] * 2,
        compiler_params=pltpu.CompilerParams(
            collective_id=collective_id, has_side_effects=True, vmem_limit_bytes=56 * 1024 * 1024
        ),
        cost_estimate=pl.CostEstimate(
            flops=2 * count * tokens * depth * units * 6,
            bytes_accessed=60 * count * tokens * units,
            transcendentals=0,
        ),
    )(a, *bs)


def table_kernel(mine_ref, all_ref, send_sem, recv_sem, own_sem):
    row, col = lax.axis_index("row"), lax.axis_index("col")
    row_count, col_count = lax.axis_size("row"), lax.axis_size("col")
    barrier = pltpu.get_barrier_semaphore()

    def col_peer(step):
        return (row, lax.rem(col + step, col_count))

    def row_peer(step):
        return (lax.rem(row + step, row_count), col)

    for step in range(1, col_count):
        pl.semaphore_signal(barrier, inc=1, device_id=col_peer(step), device_id_type=MESH)
    for step in range(1, row_count):
        pl.semaphore_signal(barrier, inc=1, device_id=row_peer(step), device_id_type=MESH)
    own = pltpu.make_async_copy(mine_ref, all_ref.at[row * col_count + col], own_sem)
    own.start()
    pl.semaphore_wait(barrier, col_count + row_count - 2)
    copies = [
        pltpu.make_async_remote_copy(
            src_ref=mine_ref,
            dst_ref=all_ref.at[row * col_count + col],
            send_sem=send_sem.at[step],
            recv_sem=recv_sem.at[step],
            device_id=col_peer(step),
            device_id_type=MESH,
        )
        for step in range(1, col_count)
    ]
    for copy in copies:
        copy.start()
    own.wait()
    for copy in copies:
        copy.wait_recv()
    held = all_ref.at[pl.ds(row * col_count, col_count)]
    onward = [
        pltpu.make_async_remote_copy(
            src_ref=held,
            dst_ref=held,
            send_sem=send_sem.at[col_count + step],
            recv_sem=recv_sem.at[col_count + step],
            device_id=row_peer(step),
            device_id_type=MESH,
        )
        for step in range(1, row_count)
    ]
    for copy in onward:
        copy.start()
    for copy in onward:
        copy.wait_recv()
    for copy in copies + onward:
        copy.wait_send()


def gather_table(local):
    row_count, col_count = lax.axis_size("row"), lax.axis_size("col")
    devices = row_count * col_count
    mine = jnp.pad(local, ((0, 0), (0, 128 - local.shape[1])))
    every = pl.pallas_call(
        table_kernel,
        out_shape=jax.ShapeDtypeStruct((devices, 1, 128), jnp.float32),
        in_specs=[pl.BlockSpec(memory_space=pltpu.VMEM)],
        out_specs=pl.BlockSpec(memory_space=pltpu.VMEM),
        scratch_shapes=[
            pltpu.SemaphoreType.DMA((row_count + col_count,)),
            pltpu.SemaphoreType.DMA((row_count + col_count,)),
            pltpu.SemaphoreType.DMA,
        ],
        compiler_params=pltpu.CompilerParams(collective_id=2, has_side_effects=True),
    )(mine)
    return every[:, 0, : local.shape[1]]


def column_sum(a, bs, collective_id):
    if lax.axis_size("col") == 4 and a.shape[0] % CHUNK == 0:
        return square_sum(a, bs, collective_id)
    dims = (((1,), (1,)), ((), ()))
    return [
        lax.psum(
            lax.dot_general(a, b, dims, preferred_element_type=jnp.float32).astype(jnp.bfloat16),
            "col",
        )
        for b in bs
    ]


def per_device(
    roll_hidden,
    roll_cotangent,
    lengths,
    owners,
    prompts,
    rewards,
    gate_weight,
    up_weight,
    down_weight,
):
    row_count = lax.axis_size("row")
    col_count = lax.axis_size("col")
    total_tokens = row_count * CAPR
    count_prompts = row_count * col_count // 8
    slot_count = roll_hidden.shape[0]
    width = roll_hidden.shape[1] // col_count
    local = jnp.stack(
        [
            lengths.astype(jnp.float32),
            owners.astype(jnp.float32),
            prompts.astype(jnp.float32),
            rewards,
        ],
        axis=1,
    )
    table = gather_table(local)
    all_lengths = table[:, 0].astype(jnp.int32)
    all_owners = table[:, 1].astype(jnp.int32)
    all_prompts = table[:, 2].astype(jnp.int32)
    weights = row_weights(all_lengths, all_prompts, table[:, 3], count_prompts)
    offsets = row_offsets(all_lengths, all_owners)
    slots = jnp.arange(slot_count, dtype=jnp.int32)
    target = jnp.where(
        slots[None, :] < all_lengths[:, None],
        all_owners[:, None] * CAPR + offsets[:, None] + slots[None, :],
        total_tokens,
    ).reshape(-1)
    slot_weights = jnp.repeat(weights, slot_count)
    pick = (jnp.arange(total_tokens, dtype=jnp.int32)[:, None] == target[None, :]).astype(
        jnp.bfloat16
    )

    def to_cols(rolled):
        blocks = rolled.reshape(slot_count, col_count, width)
        return lax.all_to_all(blocks, "col", split_axis=1, concat_axis=0, tiled=True).reshape(
            col_count * slot_count, width
        )

    def repack(every):
        return jnp.dot(pick, every, preferred_element_type=jnp.float32).astype(jnp.bfloat16)

    hidden_cols, roll_cotangent = lax.optimization_barrier((to_cols(roll_hidden), roll_cotangent))
    hidden_all = lax.all_gather(hidden_cols, "row", axis=0, tiled=True)
    cotangent_all = lax.all_gather(to_cols(roll_cotangent), "row", axis=0, tiled=True)
    packed = repack(hidden_all)
    gate, upval = column_sum(packed, (gate_weight.T, up_weight.T), 0)
    slot_weights, gate, upval = lax.optimization_barrier((slot_weights, gate, upval))
    packed_grad = repack(
        (cotangent_all.astype(jnp.float32) * slot_weights[:, None]).astype(jnp.bfloat16)
    )
    (grad_hidden,) = column_sum(packed_grad, (down_weight,), 1)
    gate, upval, grad_hidden = (v.astype(jnp.float32) for v in (gate, upval, grad_hidden))
    sig = jax.nn.sigmoid(gate)
    silu = gate * sig
    hidden = (silu * upval).astype(jnp.bfloat16)
    contract_cols = (((1,), (1,)), ((), ()))
    grad_gate_act = (grad_hidden * upval * sig * (1.0 + gate * (1.0 - sig))).astype(jnp.bfloat16)
    grad_up_act = (grad_hidden * silu).astype(jnp.bfloat16)
    contract_rows = (((0,), (0,)), ((), ()))
    grad_down = lax.dot_general(
        hidden, packed_grad, contract_rows, preferred_element_type=jnp.float32
    ).astype(jnp.bfloat16)
    grad_gate = lax.dot_general(
        packed, grad_gate_act, contract_rows, preferred_element_type=jnp.float32
    ).astype(jnp.bfloat16)
    grad_up = lax.dot_general(
        packed, grad_up_act, contract_rows, preferred_element_type=jnp.float32
    ).astype(jnp.bfloat16)
    term = lax.dot_general(
        grad_gate_act, gate_weight, contract_cols, preferred_element_type=jnp.float32
    )
    grad_input = lax.psum_scatter(
        (
            term
            + lax.dot_general(
                grad_up_act, up_weight, contract_cols, preferred_element_type=jnp.float32
            )
        ).astype(jnp.bfloat16),
        "row",
        scatter_dimension=0,
        tiled=True,
    )
    return (grad_input, grad_gate, grad_up, grad_down)


def solution(mesh):
    return jax.shard_map(
        per_device,
        mesh=mesh,
        in_specs=(
            P(("row", "col"), None),
            P(("row", "col"), None),
            P(("row", "col")),
            P(("row", "col")),
            P(("row", "col")),
            P(("row", "col")),
            P("col", "row"),
            P("col", "row"),
            P("row", "col"),
        ),
        out_specs=(P("row", "col"), P("col", "row"), P("col", "row"), P("row", "col")),
        check_vma=False,
    )
```

```python
import functools

import jax
import jax.numpy as jnp
from jax import lax
from jax.experimental import pallas as pl
from jax.experimental.pallas import tpu as pltpu
from jax.sharding import PartitionSpec as P

CAPR = 128
MESH = pl.DeviceIdType.MESH
CHUNK = 128


spread_floor = 0.7


def row_weights(lengths, prompts, rewards, count_prompts):
    onehot = (prompts[:, None] == jnp.arange(count_prompts, dtype=jnp.int32)[None, :]).astype(
        jnp.float32
    )
    counts = jnp.maximum(jnp.sum(onehot, 0), 1.0)
    means = jnp.sum(onehot * rewards[:, None], 0) / counts
    centred = rewards - jnp.sum(onehot * means[None, :], 1)
    spreads = jnp.sqrt(jnp.sum(onehot * (centred * centred)[:, None], 0) / counts)
    divisor = jnp.maximum(jnp.sum(onehot * spreads[None, :], 1), spread_floor)
    return centred / divisor / lengths.astype(jnp.float32)


def row_offsets(lengths, owners):
    count = lengths.shape[0]
    places = jnp.arange(count, dtype=jnp.int32)
    earlier = (owners[None, :] == owners[:, None]) & (places[None, :] < places[:, None])
    return jnp.sum(jnp.where(earlier, lengths[None, :], 0), 1)


def square_kernel(count, a_ref, *refs):
    b_refs, o_refs = refs[:count], refs[count : 2 * count]
    parts, first_in, second_out, second_in = (
        refs[2 * count + i * count : 3 * count + i * count] for i in range(4)
    )
    send_sem, recv_sem = refs[6 * count :]
    col = lax.axis_index("col")
    row = lax.axis_index("row")
    x, y = lax.rem(col, 2), lax.div(col, 2)
    x_peer, y_peer = y * 2 + (1 - x), (1 - y) * 2 + x
    half, quarter, eighth = CHUNK // 2, CHUNK // 4, CHUNK // 8
    ways = ((x, y, x_peer, y_peer), (y, x, y_peer, x_peer))
    chunks = a_ref.shape[0] // CHUNK

    barrier = pltpu.get_barrier_semaphore()
    for peer in (x_peer, y_peer):
        pl.semaphore_signal(barrier, inc=1, device_id=(row, peer), device_id_type=MESH)
    pl.semaphore_wait(barrier, 2)

    def rows(start, size):
        return pl.ds(pl.multiple_of(start, eighth), size)

    def copy(stage, chunk, way, i):
        f, s, f_peer, s_peer = ways[way]
        base = chunk * CHUNK + way * half
        if stage == 0:
            src = parts[i].at[rows(base + (1 - f) * quarter, quarter)]
            dst = first_in[i].at[rows(chunk * half + way * quarter, quarter)]
        elif stage == 1:
            place = rows(chunk * quarter + way * eighth, eighth)
            src, dst = second_out[i].at[place], second_in[i].at[place]
        elif stage == 2:
            place = rows(base + f * quarter + s * eighth, eighth)
            src = dst = o_refs[i].at[place]
        else:
            place = rows(base + f * quarter, quarter)
            src = dst = o_refs[i].at[place]
        return pltpu.make_async_remote_copy(
            src_ref=src,
            dst_ref=dst,
            send_sem=send_sem.at[stage, way, i, chunk],
            recv_sem=recv_sem.at[stage, way, i, chunk],
            device_id=(row, f_peer if stage in (0, 3) else s_peer),
            device_id_type=MESH,
        )

    def phase_first(chunk, carry):
        block = a_ref[rows(chunk * CHUNK, CHUNK), :]
        dims = (((1,), (1,)), ((), ()))
        for i in range(count):
            parts[i][rows(chunk * CHUNK, CHUNK), :] = lax.dot_general(
                block, b_refs[i][...], dims, preferred_element_type=jnp.float32
            ).astype(jnp.bfloat16)
            for way in range(2):
                copy(0, chunk, way, i).start()
        return carry

    def phase_second(chunk, carry):
        for i in range(count):
            for way in range(2):
                f, s = ways[way][:2]
                copy(0, chunk, way, i).wait_recv()
                mine = parts[i][
                    rows(chunk * CHUNK + way * half + f * quarter + (1 - s) * eighth, eighth), :
                ]
                other = first_in[i][
                    rows(chunk * half + way * quarter + (1 - s) * eighth, eighth), :
                ]
                second_out[i][rows(chunk * quarter + way * eighth, eighth), :] = (
                    mine.astype(jnp.float32) + other.astype(jnp.float32)
                ).astype(jnp.bfloat16)
                copy(1, chunk, way, i).start()
        return carry

    def phase_third(chunk, carry):
        for i in range(count):
            for way in range(2):
                f, s = ways[way][:2]
                copy(1, chunk, way, i).wait_recv()
                place = rows(chunk * CHUNK + way * half + f * quarter + s * eighth, eighth)
                mine = parts[i][place, :].astype(jnp.float32)
                other = first_in[i][
                    rows(chunk * half + way * quarter + s * eighth, eighth), :
                ].astype(jnp.float32)
                pair = second_in[i][rows(chunk * quarter + way * eighth, eighth), :].astype(
                    jnp.float32
                )
                o_refs[i][place, :] = (mine + other + pair).astype(jnp.bfloat16)
                copy(2, chunk, way, i).start()
        return carry

    def phase_fourth(chunk, carry):
        for i in range(count):
            for way in range(2):
                copy(2, chunk, way, i).wait_recv()
                copy(3, chunk, way, i).start()
        return carry

    def phase_last(chunk, carry):
        for i in range(count):
            for way in range(2):
                copy(3, chunk, way, i).wait_recv()
                for stage in range(4):
                    copy(stage, chunk, way, i).wait_send()
        return carry

    for phase in (phase_first, phase_second, phase_third, phase_fourth, phase_last):
        lax.fori_loop(0, chunks, phase, 0)


def square_sum(a, bs, collective_id):
    tokens, depth = a.shape
    units = bs[0].shape[0]
    count = len(bs)
    shapes = (tokens, tokens // 2, tokens // 4, tokens // 4)
    return pl.pallas_call(
        functools.partial(square_kernel, count),
        out_shape=[jax.ShapeDtypeStruct((tokens, units), jnp.bfloat16)] * count,
        in_specs=[pl.BlockSpec(memory_space=pltpu.VMEM)] * (1 + count),
        out_specs=[pl.BlockSpec(memory_space=pltpu.VMEM)] * count,
        scratch_shapes=[
            pltpu.VMEM((size, units), jnp.bfloat16) for size in shapes for _ in range(count)
        ]
        + [pltpu.SemaphoreType.DMA((4, 2, count, tokens // CHUNK))] * 2,
        compiler_params=pltpu.CompilerParams(
            collective_id=collective_id, has_side_effects=True, vmem_limit_bytes=56 * 1024 * 1024
        ),
        cost_estimate=pl.CostEstimate(
            flops=2 * count * tokens * depth * units * 6,
            bytes_accessed=60 * count * tokens * units,
            transcendentals=0,
        ),
    )(a, *bs)


def table_kernel(mine_ref, all_ref, send_sem, recv_sem, own_sem):
    row, col = lax.axis_index("row"), lax.axis_index("col")
    row_count, col_count = lax.axis_size("row"), lax.axis_size("col")
    barrier = pltpu.get_barrier_semaphore()

    def col_peer(step):
        return (row, lax.rem(col + step, col_count))

    def row_peer(step):
        return (lax.rem(row + step, row_count), col)

    for step in range(1, col_count):
        pl.semaphore_signal(barrier, inc=1, device_id=col_peer(step), device_id_type=MESH)
    for step in range(1, row_count):
        pl.semaphore_signal(barrier, inc=1, device_id=row_peer(step), device_id_type=MESH)
    own = pltpu.make_async_copy(mine_ref, all_ref.at[row * col_count + col], own_sem)
    own.start()
    pl.semaphore_wait(barrier, col_count + row_count - 2)
    copies = [
        pltpu.make_async_remote_copy(
            src_ref=mine_ref,
            dst_ref=all_ref.at[row * col_count + col],
            send_sem=send_sem.at[step],
            recv_sem=recv_sem.at[step],
            device_id=col_peer(step),
            device_id_type=MESH,
        )
        for step in range(1, col_count)
    ]
    for copy in copies:
        copy.start()
    own.wait()
    for copy in copies:
        copy.wait_recv()
    held = all_ref.at[pl.ds(row * col_count, col_count)]
    onward = [
        pltpu.make_async_remote_copy(
            src_ref=held,
            dst_ref=held,
            send_sem=send_sem.at[col_count + step],
            recv_sem=recv_sem.at[col_count + step],
            device_id=row_peer(step),
            device_id_type=MESH,
        )
        for step in range(1, row_count)
    ]
    for copy in onward:
        copy.start()
    for copy in onward:
        copy.wait_recv()
    for copy in copies + onward:
        copy.wait_send()


def gather_table(local):
    row_count, col_count = lax.axis_size("row"), lax.axis_size("col")
    devices = row_count * col_count
    mine = jnp.pad(local, ((0, 0), (0, 128 - local.shape[1])))
    every = pl.pallas_call(
        table_kernel,
        out_shape=jax.ShapeDtypeStruct((devices, 1, 128), jnp.float32),
        in_specs=[pl.BlockSpec(memory_space=pltpu.VMEM)],
        out_specs=pl.BlockSpec(memory_space=pltpu.VMEM),
        scratch_shapes=[
            pltpu.SemaphoreType.DMA((row_count + col_count,)),
            pltpu.SemaphoreType.DMA((row_count + col_count,)),
            pltpu.SemaphoreType.DMA,
        ],
        compiler_params=pltpu.CompilerParams(collective_id=2, has_side_effects=True),
    )(mine)
    return every[:, 0, : local.shape[1]]


def column_sum(a, bs, collective_id):
    if lax.axis_size("col") == 4 and a.shape[0] % CHUNK == 0:
        return square_sum(a, bs, collective_id)
    dims = (((1,), (1,)), ((), ()))
    return [
        lax.psum(
            lax.dot_general(a, b, dims, preferred_element_type=jnp.float32).astype(jnp.bfloat16),
            "col",
        )
        for b in bs
    ]


def per_device(
    roll_hidden,
    roll_cotangent,
    lengths,
    owners,
    prompts,
    rewards,
    gate_weight,
    up_weight,
    down_weight,
):
    row_count = lax.axis_size("row")
    col_count = lax.axis_size("col")
    total_tokens = row_count * CAPR
    count_prompts = row_count * col_count // 8
    slot_count = roll_hidden.shape[0]
    width = roll_hidden.shape[1] // col_count
    local = jnp.stack(
        [
            lengths.astype(jnp.float32),
            owners.astype(jnp.float32),
            prompts.astype(jnp.float32),
            rewards,
        ],
        axis=1,
    )
    table = gather_table(local)
    all_lengths = table[:, 0].astype(jnp.int32)
    all_owners = table[:, 1].astype(jnp.int32)
    all_prompts = table[:, 2].astype(jnp.int32)
    weights = row_weights(all_lengths, all_prompts, table[:, 3], count_prompts)
    offsets = row_offsets(all_lengths, all_owners)
    starts = jnp.cumsum(all_lengths) - all_lengths
    live_total = jnp.sum(all_lengths)
    slots = jnp.arange(slot_count, dtype=jnp.int32)
    target = jnp.where(
        slots[None, :] < all_lengths[:, None], starts[:, None] + slots[None, :], total_tokens
    ).reshape(-1)
    slot_weights = jnp.repeat(weights, slot_count)
    firsts = all_owners * CAPR + offsets
    places = jnp.arange(total_tokens, dtype=jnp.int32)[:, None]
    inside = (places >= firsts[None, :]) & (places < (firsts + all_lengths)[None, :])
    held_at = jnp.sum(jnp.where(inside, places + (starts - firsts + 1)[None, :], 0), 1) - 1

    def to_cols(rolled):
        blocks = rolled.reshape(slot_count, col_count, width)
        return lax.all_to_all(blocks, "col", split_axis=1, concat_axis=0, tiled=True).reshape(
            col_count * slot_count, width
        )

    hidden_cols, roll_cotangent = lax.optimization_barrier((to_cols(roll_hidden), roll_cotangent))
    hidden_all = lax.all_gather(hidden_cols, "row", axis=0, tiled=True)
    operands = (
        hidden_all,
        to_cols(roll_cotangent),
        target,
        slot_weights,
        held_at,
        gate_weight,
        up_weight,
        down_weight,
    )
    fewer = total_tokens * 7 // 8
    return lax.cond(
        live_total <= fewer,
        functools.partial(layer, fewer, total_tokens, 0),
        functools.partial(layer, total_tokens, total_tokens, 3),
        *operands,
    )


def layer(
    tokens,
    total_tokens,
    first_id,
    hidden_all,
    cotangent_cols,
    target,
    slot_weights,
    held_at,
    gate_weight,
    up_weight,
    down_weight,
):
    ids = jnp.arange(tokens, dtype=jnp.int32)
    pick = (ids[:, None] == target[None, :]).astype(jnp.bfloat16)
    spread_out = (held_at[:, None] == ids[None, :]).astype(jnp.bfloat16)

    def move(onehot, every):
        return jnp.dot(onehot, every, preferred_element_type=jnp.float32).astype(jnp.bfloat16)

    cotangent_all = lax.all_gather(cotangent_cols, "row", axis=0, tiled=True)
    packed = move(pick, hidden_all)
    gate, upval = column_sum(packed, (gate_weight.T, up_weight.T), first_id)
    slot_weights, gate, upval = lax.optimization_barrier((slot_weights, gate, upval))
    packed_grad = move(
        pick, (cotangent_all.astype(jnp.float32) * slot_weights[:, None]).astype(jnp.bfloat16)
    )
    (grad_hidden,) = column_sum(packed_grad, (down_weight,), first_id + 1)
    gate, upval, grad_hidden = (v.astype(jnp.float32) for v in (gate, upval, grad_hidden))
    sig = jax.nn.sigmoid(gate)
    silu = gate * sig
    hidden = (silu * upval).astype(jnp.bfloat16)
    contract_cols = (((1,), (1,)), ((), ()))
    grad_gate_act = (grad_hidden * upval * sig * (1.0 + gate * (1.0 - sig))).astype(jnp.bfloat16)
    grad_up_act = (grad_hidden * silu).astype(jnp.bfloat16)
    contract_rows = (((0,), (0,)), ((), ()))
    grad_down = lax.dot_general(
        hidden, packed_grad, contract_rows, preferred_element_type=jnp.float32
    ).astype(jnp.bfloat16)
    grad_gate = lax.dot_general(
        packed, grad_gate_act, contract_rows, preferred_element_type=jnp.float32
    ).astype(jnp.bfloat16)
    grad_up = lax.dot_general(
        packed, grad_up_act, contract_rows, preferred_element_type=jnp.float32
    ).astype(jnp.bfloat16)
    term = lax.dot_general(
        grad_gate_act, gate_weight, contract_cols, preferred_element_type=jnp.float32
    )
    term = (
        term
        + lax.dot_general(
            grad_up_act, up_weight, contract_cols, preferred_element_type=jnp.float32
        )
    ).astype(jnp.bfloat16)
    grad_input = lax.psum_scatter(
        move(spread_out, term), "row", scatter_dimension=0, tiled=True
    )
    return (grad_input, grad_gate, grad_up, grad_down)


def solution(mesh):
    return jax.shard_map(
        per_device,
        mesh=mesh,
        in_specs=(
            P(("row", "col"), None),
            P(("row", "col"), None),
            P(("row", "col")),
            P(("row", "col")),
            P(("row", "col")),
            P(("row", "col")),
            P("col", "row"),
            P("col", "row"),
            P("row", "col"),
        ),
        out_specs=(P("row", "col"), P("col", "row"), P("col", "row"), P("row", "col")),
        check_vma=False,
    )
```
